512 devices in a mesh: frames: 8 (over z_lo), slabs: 64 (over y, x, z_hi, core).
Axes of the slice: x: 4, y: 4, z: 16 (z_hi: 2, z_lo: 8; z = z_hi * 8 + z_lo), core: 2. Of those that a mesh axis runs over, the one named last changes fastest.
Arguments:
- movie: bfloat16 [64, 131072], P('frames', 'slabs'), may hold values from -48 to 48
- traces: bfloat16 [64, 1024], P('frames', 'slabs'), may hold values from -6 to 6
- voxel_index: int32 [1024, 2048], P('slabs'), may hold values from 0 to 4095, as said below
- footprint: float32 [1024, 2048], P('slabs'), may hold values from 0 to 1
- block_order: int32 [2], replicated, may hold values from 0 to 1, each once
Outputs:
- updated: float32 [1024, 2048], P('slabs')
The draws below stay inside these ranges and needn't reach their ends.
Inputs may be any that keep to these rules, and one draw needn't show every extreme that they name: `voxel_index`: within a row all 2048 positions are distinct and lie in a run of 4096 consecutive positions, whose first and last position are both in the row.
All inputs are finite; a program needn't handle non-finite values.
Results may differ from the reference program's by a relative error of at most 0.0003.
Values may be sent and summed in bfloat16 or wider, within the bound.
No kernel may reach another device: no remote copies, remote signals or barrier semaphores. Data moves between devices by JAX's collectives and lax.ppermute only.
A program may use at most 64 MiB of HBM per device.

```python
import jax
import jax.numpy as jnp
from jax import lax

VOXEL_DEV = 2048
SOURCE_DEV = 16
FOOTPRINT = 2048
BLOCK_SIZE = 8
SWEEPS = 2
WINDOW = 4096
MARGIN = 1024
EXTENT = 4096
BLOCKS = 2
FRAMES = 64
VOXELS = 131072
SOURCES = 1024
N_SLABS = 64


def draw_voxel_index(key, part):
    keys = jax.random.split(jax.random.fold_in(key, 7), SOURCES)

    def one_row(row_key):
        return jax.random.permutation(row_key, WINDOW - 2)[:FOOTPRINT - 2]
    inner = jax.vmap(one_row)(keys)
    offset = jax.random.randint(jax.random.fold_in(key, 11), (SOURCES,), 0, EXTENT - WINDOW + 1)
    within = jnp.arange(SOURCES) % SOURCE_DEV
    offset = jnp.where(within == 0, 0, jnp.where(within == 1, EXTENT - WINDOW, offset))
    first = offset[:, None]
    last = offset[:, None] + WINDOW - 1
    return jnp.concatenate([first, last, offset[:, None] + 1 + inner], axis=1).astype(jnp.int32)


def shard_levels(rng, dims, shards, least, high):
    def one(position, shards_of):
        steps = jax.random.uniform(jax.random.fold_in(jax.random.fold_in(rng, 6), position), (shards_of,), jnp.float32, least / len(shards), high / len(shards))
        return jnp.repeat(jnp.exp(steps), dims[position] // shards_of).reshape((-1,) + (1,) * (len(dims) - position - 1))

    factor_of = one(*shards[0])
    for cut in shards[1:]:
        factor_of = factor_of * one(*cut)
    return factor_of


def normal_values(rng, extent, spread, most, cuts=(), held_as=jnp.bfloat16):
    gain = shard_levels(rng, extent, cuts, -0.22, 0.18) if cuts else 1.0
    entries = jax.random.normal(rng, extent, jnp.float32) * spread * gain
    return jnp.minimum(jnp.maximum(entries, -most), most).astype(held_as)


def setup_inputs(seed: int = 0) -> dict:
    key_list = jax.random.split(jax.random.key(seed), 6)
    return {
        "movie": normal_values(key_list[0], (FRAMES, VOXELS), 8.0, 48.0, ((0, 8), (1, 64))),
        "traces": normal_values(key_list[1], (FRAMES, SOURCES), 1.0, 6.0, ((0, 8), (1, 64))),
        "voxel_index": draw_voxel_index(jax.random.fold_in(key_list[5], 71), 0),
        "footprint": jnp.clip(1.0 * jax.random.uniform(key_list[3], (SOURCES, FOOTPRINT), jnp.float32) ** shard_levels(key_list[3], (SOURCES, FOOTPRINT), ((0, 64),), -0.2, 0.2), 0.0, 1.0),
        "block_order": jax.random.permutation(key_list[4], BLOCKS).astype(jnp.int32),
    }


def transposed(left, right):
    return lax.dot_general(left, right, (((0,), (0,)), ((), ())), preferred_element_type=jnp.float32)


def sweep_blocks(current, left_rows, right_rows, stat, gram, support, block_order):
    diagonal = jnp.diagonal(gram[:, SOURCE_DEV:2 * SOURCE_DEV]) + 1.0

    def one_block(state, blk):
        start = (blk * BLOCK_SIZE).astype(jnp.int32)
        g_rows = lax.dynamic_slice_in_dim(gram, start, BLOCK_SIZE, 0)
        every = jnp.concatenate([left_rows, state, right_rows], axis=0)
        pulled = jnp.dot(g_rows, every, precision=lax.Precision.HIGHEST, preferred_element_type=jnp.float32)
        old = lax.dynamic_slice_in_dim(state, start, BLOCK_SIZE, 0)
        stat_rows = lax.dynamic_slice_in_dim(stat, start, BLOCK_SIZE, 0)
        mask_rows = lax.dynamic_slice_in_dim(support, start, BLOCK_SIZE, 0)
        scale = lax.dynamic_slice_in_dim(diagonal, start, BLOCK_SIZE, 0)
        fresh = mask_rows * jnp.maximum(old + (stat_rows - pulled) / scale[:, None], 0.0)
        return lax.dynamic_update_slice_in_dim(state, fresh, start, 0), None

    result, unused = lax.scan(one_block, current, block_order)
    return result


def reference(movie, traces, voxel_index, footprint, block_order):
    padded = jnp.pad(movie, ((0, 0), (MARGIN, MARGIN)))
    blank_traces = jnp.zeros((FRAMES, SOURCE_DEV), traces.dtype)
    trace_pad = jnp.concatenate([blank_traces, traces, blank_traces], axis=1)
    slab_ids = jnp.arange(N_SLABS).astype(jnp.int32)
    index_slabs = voxel_index.reshape(N_SLABS, SOURCE_DEV, FOOTPRINT)
    value_slabs = footprint.reshape(N_SLABS, SOURCE_DEV, FOOTPRINT)
    rows = jnp.arange(SOURCE_DEV)[:, None]

    def statistics(slab):
        extended = lax.dynamic_slice_in_dim(padded, (slab * VOXEL_DEV).astype(jnp.int32), EXTENT, 1)
        nearby = lax.dynamic_slice_in_dim(trace_pad, (slab * SOURCE_DEV).astype(jnp.int32), 3 * SOURCE_DEV, 1)
        own = nearby[:, SOURCE_DEV:2 * SOURCE_DEV]
        return transposed(own, extended), transposed(own, nearby)

    stat, gram = lax.map(statistics, slab_ids)

    def build(pair):
        index_rows, value_rows = pair
        dense = jnp.zeros((SOURCE_DEV, EXTENT), jnp.float32).at[rows, index_rows].set(value_rows)
        support = jnp.zeros((SOURCE_DEV, EXTENT), jnp.float32).at[rows, index_rows].set(1.0)
        return dense, support

    dense, support = lax.map(build, (index_slabs, value_slabs))
    blank_half = jnp.zeros((SOURCE_DEV, VOXEL_DEV), jnp.float32)
    for sweep in range(SWEEPS):
        blank_slab = jnp.zeros((1, SOURCE_DEV, EXTENT), jnp.float32)
        widened = jnp.concatenate([blank_slab, dense, blank_slab], axis=0)

        def update(slab):
            before = lax.dynamic_index_in_dim(widened, slab, 0, keepdims=False)
            here = lax.dynamic_index_in_dim(widened, slab + 1, 0, keepdims=False)
            after = lax.dynamic_index_in_dim(widened, slab + 2, 0, keepdims=False)
            left_rows = jnp.concatenate([before[:, VOXEL_DEV:], blank_half], axis=1)
            right_rows = jnp.concatenate([blank_half, after[:, :VOXEL_DEV]], axis=1)
            return sweep_blocks(here, left_rows, right_rows, stat[slab], gram[slab], support[slab], block_order)

        dense = lax.map(update, slab_ids)

    def pick(pair):
        state, index_rows = pair
        return state[rows, index_rows]

    picked = lax.map(pick, (dense, index_slabs))
    return picked.reshape(SOURCES, FOOTPRINT)
```

```python
import functools

import jax
import jax.numpy as jnp
from jax import lax
from jax.experimental import pallas as pl
from jax.experimental.pallas import tpu as pltpu
from jax.sharding import PartitionSpec as P

F32 = jnp.float32
BF16 = jnp.bfloat16
BLOCK = 8
LANES = 128
FAR = 4


def scatter_kernel(idx_ref, val_ref, out_ref, rows_ref):
    sources, count = idx_ref.shape
    tiles = out_ref.shape[1] // LANES
    tile_ids = lax.broadcasted_iota(jnp.int32, (tiles, count), 0)
    lane_ids = lax.broadcasted_iota(jnp.int32, (LANES, count), 0)
    for k in range(sources):
        pos = idx_ref[k : k + 1, :]
        val = val_ref[k : k + 1, :]
        top = val.astype(BF16).astype(F32)
        rest = val - top
        mid = rest.astype(BF16).astype(F32)
        low = rest - mid
        in_tile = tile_ids == (pos >> 7)
        on_lane = (lane_ids == (pos & (LANES - 1))).astype(F32).astype(BF16)
        left = jnp.concatenate(
            [
                jnp.where(in_tile, part, 0.0)
                for part in (top, mid, low, jnp.ones_like(val))
            ],
            axis=0,
        ).astype(BF16)
        found = lax.dot_general(
            left, on_lane, (((1,), (1,)), ((), ())), preferred_element_type=F32
        )
        value = found[:tiles] + (found[tiles : 2 * tiles] + found[2 * tiles : 3 * tiles])
        rows_ref[k * tiles : (k + 1) * tiles, :] = jnp.where(
            found[3 * tiles :] > 0.5, value, -1.0
        )
    for t in range(tiles):
        out_ref[:, t * LANES : (t + 1) * LANES] = rows_ref[pl.ds(t, sources, stride=tiles), :]


def scatter(voxel_index, footprint, extent):
    sources, _ = voxel_index.shape
    return pl.pallas_call(
        scatter_kernel,
        out_shape=jax.ShapeDtypeStruct((sources, extent), F32),
        scratch_shapes=[pltpu.VMEM((sources * extent // LANES, LANES), F32)],
        cost_estimate=pl.CostEstimate(flops=8_000_000_000, bytes_accessed=524288, transcendentals=0),
    )(voxel_index, footprint)


def parts_of(x):
    top = x.astype(BF16).astype(F32)
    return top, x - top


def weights(g):
    top, low = parts_of(g)
    packed = top + pltpu.roll(low, 32, 1) + pltpu.roll(top, 64, 1) + pltpu.roll(low, 96, 1)
    return packed.astype(BF16)


def pull(packed, x):
    top, low = parts_of(x)
    top, low = top.astype(BF16), low.astype(BF16)
    stacked = jnp.concatenate([top, top, low, low], axis=0)
    return jnp.dot(packed, stacked, preferred_element_type=F32)


def sweep_kernel(far_ref, order_ref, data_ref, own_ref, low_ref, high_ref, idx_ref, out_ref,
                 movie_ref, turned_ref, dense_ref):
    groups, pairs, rows, _ = data_ref.shape
    frames = groups * pairs * rows
    sources, extent = own_ref.shape
    half = extent // 2
    margin = half // 2
    far_low, far_high = far_ref[0], far_ref[1]

    lane = lax.broadcasted_iota(jnp.int32, (rows, LANES), 1)
    pieces = []
    for g in range(groups):
        for b in range(pairs):
            at = (g * pairs + b) * rows
            lo = b ^ far_low
            hi = b ^ far_high
            movie_ref[at : at + rows, :margin] = data_ref[g, lo, :, :margin].astype(F32)
            movie_ref[at : at + rows, margin : 3 * margin] = data_ref[g, b, :, margin : 3 * margin].astype(F32)
            movie_ref[at : at + rows, 3 * margin :] = data_ref[g, hi, :, 3 * margin : extent].astype(F32)
            pieces.append(
                jnp.where(
                    lane < sources,
                    data_ref[g, lo, :, extent:].astype(F32),
                    jnp.where(
                        lane < 2 * sources,
                        data_ref[g, b, :, extent:].astype(F32),
                        data_ref[g, hi, :, extent:].astype(F32),
                    ),
                )
            )
    turned_ref[...] = jnp.transpose(jnp.concatenate(pieces, axis=0))
    first = pl.multiple_of(order_ref[0] * BLOCK, BLOCK)
    second = pl.multiple_of(order_ref[1] * BLOCK, BLOCK)
    turned = jnp.concatenate(
        [turned_ref[pl.ds(base + at, BLOCK), :] for base in (0, sources, 2 * sources) for at in (first, second)]
        + [jnp.zeros((LANES - 3 * sources, frames), F32)],
        axis=0,
    ).astype(BF16)
    gram = lax.dot_general(turned, turned, (((1,), (1,)), ((), ())), preferred_element_type=F32)
    here = lax.broadcasted_iota(jnp.int32, (LANES, LANES), 0)
    there = lax.broadcasted_iota(jnp.int32, (LANES, LANES), 1)
    scale = jnp.sum(jnp.where(here == there, gram, 0.0), axis=1, keepdims=True) + 1.0
    inverse = 1.0 / scale

    def fresh(old, held, stat, pulled, inv):
        return jnp.where(held, jnp.maximum(old + (stat - pulled) * inv, 0.0), 0.0)

    live = lax.broadcasted_iota(jnp.int32, (2 * sources, LANES), 1) < 2 * sources
    for side in range(2):
        base = side * sources
        cols = pl.ds(side * half, half)
        g = gram[base : base + 2 * sources]
        if side:
            g = pltpu.roll(g, LANES - base, 1)
        g = jnp.where(live, g, 0.0)
        inv = inverse[base : base + 2 * sources]
        stat = jnp.dot(
            turned[base : base + 2 * sources],
            movie_ref[:, cols].astype(BF16),
            preferred_element_type=F32,
        )
        near_ref = high_ref if side else low_ref
        mine = [own_ref[pl.ds(at, BLOCK), cols] for at in (first, second)]
        near = [near_ref[pl.ds(at, BLOCK), :] for at in (first, second)]
        raw = mine + near if side else near + mine
        held = [r >= 0.0 for r in raw]
        x = [jnp.maximum(r, 0.0) for r in raw]
        s = [stat[i * BLOCK : (i + 1) * BLOCK] for i in range(4)]
        v = [inv[i * BLOCK : (i + 1) * BLOCK] for i in range(4)]
        packed = weights(g)
        inside = jnp.where(
            (lax.broadcasted_iota(jnp.int32, g.shape, 0) // sources)
            == (lax.broadcasted_iota(jnp.int32, g.shape, 1) // sources),
            g,
            0.0,
        )
        inside = weights(inside)
        zero = jnp.zeros_like(x[0])
        p = pull(packed, jnp.concatenate(x, axis=0))
        p = [p[i * BLOCK : (i + 1) * BLOCK] for i in range(4)]
        new = list(x)
        for i in (0, 2):
            new[i] = fresh(x[i], held[i], s[i], p[i], v[i])
        more = pull(inside, jnp.concatenate([new[0] - x[0], zero, new[2] - x[2], zero], axis=0))
        for i in (1, 3):
            new[i] = fresh(x[i], held[i], s[i], p[i] + more[i * BLOCK : (i + 1) * BLOCK], v[i])
        a = 0 if side else 2
        p = pull(packed, jnp.concatenate(new, axis=0))
        last = fresh(new[a], held[a], s[a], p[a * BLOCK : (a + 1) * BLOCK], v[a])
        change = [zero] * 4
        change[a] = last - new[a]
        more = pull(inside, jnp.concatenate(change, axis=0))
        b = a + 1
        rows_b = slice(b * BLOCK, (b + 1) * BLOCK)
        final = fresh(new[b], held[b], s[b], p[rows_b] + more[rows_b], v[b])
        dense_ref[pl.ds(first, BLOCK), cols] = last
        dense_ref[pl.ds(second, BLOCK), cols] = final

    for r in range(0, sources, BLOCK):
        table = [dense_ref[r : r + BLOCK, t * LANES : (t + 1) * LANES] for t in range(extent // LANES)]
        for c in range(0, idx_ref.shape[1], LANES):
            pos = idx_ref[r : r + BLOCK, c : c + LANES]
            tile = pos >> 7
            at = pos & (LANES - 1)
            got = jnp.zeros((BLOCK, LANES), F32)
            for t in range(extent // LANES):
                got = jnp.where(tile == t, jnp.take_along_axis(table[t], at, axis=1), got)
            out_ref[r : r + BLOCK, c : c + LANES] = got


def sweeps(far, order, data, own, low, high, voxel_index):
    sources, extent = own.shape
    groups, pairs, rows, _ = data.shape
    smem = pl.BlockSpec(memory_space=pltpu.SMEM)
    vmem = pl.BlockSpec(memory_space=pltpu.VMEM)
    return pl.pallas_call(
        sweep_kernel,
        out_shape=jax.ShapeDtypeStruct(voxel_index.shape, F32),
        in_specs=[smem, smem] + [vmem] * 5,
        out_specs=vmem,
        scratch_shapes=[
            pltpu.VMEM((groups * pairs * rows, extent), F32),
            pltpu.VMEM((LANES, groups * pairs * rows), F32),
            pltpu.VMEM((sources, extent), F32),
        ],
    )(far, order, data, own, low, high, voxel_index)


def joint(frames, slabs, step):
    pairs = []
    for f in range(frames):
        for s in range(slabs):
            if 0 <= s + step < slabs:
                odd = s % 2 if step > 0 else (s + 1) % 2
                pairs.append((f * slabs + s, (f ^ (FAR * odd)) * slabs + s + step))
    return pairs


def local(sizes, movie, traces, voxel_index, footprint, block_order):
    frames, slabs = sizes
    both = ("frames", "slabs")
    up, down = joint(frames, slabs, 1), joint(frames, slabs, -1)
    voxels = movie.shape[1]
    half = voxels // 2
    sources = traces.shape[1]
    extent = 2 * voxels
    padded = jnp.pad(traces, ((0, 0), (0, LANES - sources)))
    low = lax.ppermute(jnp.concatenate([movie[:, half:], padded], axis=1), both, up)
    high = lax.ppermute(jnp.concatenate([movie[:, :half], padded], axis=1), both, down)
    dense = scatter(voxel_index, footprint, extent)
    low_dense = lax.ppermute(dense[:, voxels:], both, up)
    high_dense = lax.ppermute(dense[:, :voxels], both, down)
    mine = jnp.concatenate(
        [
            low[:, :half], movie, high[:, :half],
            low[:, half : half + sources], traces, high[:, half : half + sources],
            jnp.zeros((movie.shape[0], LANES - 3 * sources), movie.dtype),
        ],
        axis=1,
    )
    other = lax.ppermute(mine, "frames", [(f, f ^ FAR) for f in range(frames)])
    pair = jnp.stack([mine, other])
    data = lax.all_to_all(
        jnp.broadcast_to(pair[None], (FAR,) + pair.shape), "frames", 0, 0,
        axis_index_groups=[list(range(a, a + FAR)) for a in range(0, frames, FAR)],
    )
    odd = lax.rem(lax.axis_index("slabs"), 2)
    far = jnp.stack([1 - odd, odd]).astype(jnp.int32)
    return sweeps(far, block_order, data, dense, low_dense, high_dense, voxel_index)


def solution(mesh):
    sizes = (mesh.shape["frames"], mesh.shape["slabs"])
    in_specs = (P("frames", "slabs"), P("frames", "slabs"), P("slabs", None), P("slabs", None), P())
    return jax.shard_map(
        functools.partial(local, sizes), mesh=mesh, in_specs=in_specs,
        out_specs=P("slabs", None), check_vma=False,
    )
```

```python
import functools

import jax
import jax.numpy as jnp
from jax import lax
from jax.experimental import pallas as pl
from jax.experimental.pallas import tpu as pltpu
from jax.sharding import PartitionSpec as P

F32 = jnp.float32
BF16 = jnp.bfloat16
BLOCK = 8
LANES = 128
FAR = 4


def call(body, out_shape, scalars, arrays, scratch=(), limit=16):
    vmem = pl.BlockSpec(memory_space=pltpu.VMEM)
    smem = pl.BlockSpec(memory_space=pltpu.SMEM)
    return pl.pallas_call(
        body,
        out_shape=out_shape,
        in_specs=[smem] * len(scalars) + [vmem] * len(arrays),
        out_specs=jax.tree.map(lambda _: vmem, out_shape),
        scratch_shapes=list(scratch),
        compiler_params=pltpu.CompilerParams(vmem_limit_bytes=limit << 20),
    )(*scalars, *arrays)


def thirds(x):
    top = x.astype(BF16).astype(F32)
    rest = x - top
    mid = rest.astype(BF16).astype(F32)
    return top, mid, rest - mid


def front_kernel(where_ref, idx_ref, val_ref, movie_ref, traces_ref, out_ref, far_ref, near_ref, rows_ref):
    sources, count = idx_ref.shape
    tiles = 2 * far_ref.shape[1] // LANES
    odd, frame = where_ref[0], where_ref[1]
    tile_ids = lax.broadcasted_iota(jnp.int32, (tiles, count), 0)
    lane_ids = lax.broadcasted_iota(jnp.int32, (LANES, count), 0)
    for k in range(sources):
        pos = idx_ref[k : k + 1, :]
        val = val_ref[k : k + 1, :]
        in_tile = tile_ids == (pos >> 7)
        on_lane = (lane_ids == (pos & (LANES - 1))).astype(F32).astype(BF16)
        left = jnp.concatenate(
            [jnp.where(in_tile, part, 0.0) for part in thirds(val) + (jnp.ones_like(val),)], axis=0
        ).astype(BF16)
        found = lax.dot_general(left, on_lane, (((1,), (1,)), ((), ())), preferred_element_type=F32)
        value = found[:tiles] + (found[tiles : 2 * tiles] + found[2 * tiles : 3 * tiles])
        rows_ref[k * tiles : (k + 1) * tiles, :] = jnp.where(found[3 * tiles :] > 0.5, value, -1.0)
    for t in range(tiles // 2):
        cols = slice(t * LANES, (t + 1) * LANES)
        left = rows_ref[pl.ds(t, sources, stride=tiles), :]
        right = rows_ref[pl.ds(t + tiles // 2, sources, stride=tiles), :]
        far_ref[:, cols] = jnp.where(odd == 1, right, left)
        near_ref[:, cols] = jnp.where(odd == 1, left, right)

    rows, voxels = movie_ref.shape
    half = voxels // 2
    share = far_ref.shape[1] // 8
    at = odd * half
    far_half = movie_ref[:, pl.ds(pl.multiple_of(at, half), half)]
    near_half = movie_ref[:, pl.ds(pl.multiple_of(half - at, half), half)]
    tail = jnp.concatenate(
        [traces_ref[...].astype(F32), jnp.zeros((rows, LANES - sources), F32)], axis=1
    ).astype(BF16)
    piece = far_ref[:, pl.ds(pl.multiple_of(frame * share, share), share)]
    parts = [p[r : r + rows].astype(BF16) for p in parts_of(piece) for r in range(0, sources, rows)]
    mine = 2 * (1 - odd)
    for h in range(2):
        for slot in (mine + h, 2 - mine + h):
            out_ref[slot, :, :half] = far_half
            out_ref[slot, :, half : half + LANES] = tail
        out_ref[mine + h, :, half + LANES : 2 * half + LANES] = near_half
        for i, part in enumerate(parts):
            out_ref[2 - mine + h, :, pl.ds(half + LANES + i * share, share)] = part


def middle_kernel(where_ref, in_ref, out_ref):
    rows = in_ref.shape[1]
    half = (out_ref.shape[3] - in_ref.shape[2]) // 2
    odd, live = where_ref[0], where_ref[2]
    mine = 2 * (1 - odd)
    lane = lax.broadcasted_iota(jnp.int32, (rows, LANES), 1)
    for h in range(2):
        own, far = mine + h, 2 - mine + h
        far_half = in_ref[far, :, :half].astype(F32)
        far_half = jnp.where(live == 1, far_half, 0.0).astype(BF16)
        far_tail = jnp.where(live == 1, in_ref[far, :, half : half + LANES].astype(F32), 0.0)
        tail = (far_tail + pltpu.roll(in_ref[own, :, half : half + LANES].astype(F32), 16, 1)).astype(BF16)
        own_far = in_ref[own, :, :half]
        own_near = in_ref[own, :, half + LANES : 2 * half + LANES]
        dense = in_ref[far, :, half + LANES :]
        for g in range(FAR):
            out_ref[g, h, :, :half] = far_half
            out_ref[g, h, :, half : 2 * half] = own_far
            out_ref[g, h, :, 2 * half : 3 * half] = own_near
            out_ref[g, h, :, 3 * half : 3 * half + LANES] = tail
            out_ref[g, h, :, 3 * half + LANES :] = dense


def near_kernel(data_ref, dense_ref, out_ref):
    groups, pairs, rows, width = out_ref.shape
    sources, side = dense_ref.shape
    half = side // 2
    share = width - half - LANES
    for g in range(groups):
        for h in range(pairs):
            out_ref[g, h, :, :half] = data_ref[g, h, :, 2 * half : 3 * half].astype(F32)
            tail = data_ref[g, h, :, 3 * half : 3 * half + LANES].astype(F32)
            out_ref[g, h, :, half : half + LANES] = pltpu.roll(tail, LANES - 16, 1)
            out_ref[g, h, :, half + LANES :] = dense_ref[h * rows : (h + 1) * rows, g * share : (g + 1) * share]


def parts_of(x):
    top = x.astype(BF16).astype(F32)
    return top, x - top


def weights(g):
    top, low = parts_of(g)
    packed = top + pltpu.roll(low, 32, 1) + pltpu.roll(top, 64, 1) + pltpu.roll(low, 96, 1)
    return packed.astype(BF16)


def pull(packed, x):
    top, low = parts_of(x)
    top, low = top.astype(BF16), low.astype(BF16)
    stacked = jnp.concatenate([top, top, low, low], axis=0)
    return jnp.dot(packed, stacked, preferred_element_type=F32)


def both_sweeps(order_ref, tails, movie_ref, turned_ref, own_ref, other_ref, final_ref):
    sources = own_ref.shape[0]
    frames = movie_ref.shape[0]
    turned_ref[...] = jnp.transpose(jnp.concatenate(tails, axis=0))
    first = pl.multiple_of(order_ref[0] * BLOCK, BLOCK)
    second = pl.multiple_of(order_ref[1] * BLOCK, BLOCK)
    turned = jnp.concatenate(
        [turned_ref[pl.ds(base + at, BLOCK), :] for base in (0, sources) for at in (first, second)]
        + [jnp.zeros((LANES - 2 * sources, frames), F32)],
        axis=0,
    ).astype(BF16)
    gram = lax.dot_general(turned, turned, (((1,), (1,)), ((), ())), preferred_element_type=F32)[: 2 * sources]
    here = lax.broadcasted_iota(jnp.int32, gram.shape, 0)
    there = lax.broadcasted_iota(jnp.int32, gram.shape, 1)
    inverse = 1.0 / (jnp.sum(jnp.where(here == there, gram, 0.0), axis=1, keepdims=True) + 1.0)
    packed = weights(gram)
    inside = weights(jnp.where(here // sources == there // sources, gram, 0.0))
    stat = jnp.dot(turned[: 2 * sources], movie_ref[...].astype(BF16), preferred_element_type=F32)

    def cut(a):
        return [a[i * BLOCK : (i + 1) * BLOCK] for i in range(a.shape[0] // BLOCK)]

    raw = [ref[pl.ds(at, BLOCK), :] for ref in (other_ref, own_ref) for at in (first, second)]
    held = [r >= 0.0 for r in raw]
    x = [jnp.maximum(r, 0.0) for r in raw]
    s, v = cut(stat), cut(inverse)
    zero = jnp.zeros_like(x[0])

    def fresh(i, old, pulled):
        return jnp.where(held[i], jnp.maximum(old + (s[i] - pulled) * v[i], 0.0), 0.0)

    p = cut(pull(packed, jnp.concatenate(x, axis=0)))
    new = list(x)
    for i in (0, 2):
        new[i] = fresh(i, x[i], p[i])
    more = cut(pull(inside, jnp.concatenate([new[0] - x[0], zero, new[2] - x[2], zero], axis=0)))
    for i in (1, 3):
        new[i] = fresh(i, x[i], p[i] + more[i])
    p = cut(pull(packed[2 * BLOCK :], jnp.concatenate(new, axis=0)))
    last = fresh(2, new[2], p[0])
    more = pull(inside[3 * BLOCK :], jnp.concatenate([zero, zero, last - new[2], zero], axis=0))
    final = fresh(3, new[3], p[1] + more)
    final_ref[pl.ds(first, BLOCK), :] = last
    final_ref[pl.ds(second, BLOCK), :] = final


def pick(final_ref, idx_ref, out_ref, flip, base, start_ref):
    sources, half = final_ref.shape
    for r in range(0, sources, BLOCK):
        table = [final_ref[r : r + BLOCK, t * LANES : (t + 1) * LANES] for t in range(half // LANES)]
        for c in range(0, idx_ref.shape[1], LANES):
            pos = idx_ref[r : r + BLOCK, c : c + LANES] ^ flip
            tile = (pos >> 7) - base
            at = pos & (LANES - 1)
            got = jnp.zeros((BLOCK, LANES), F32) if start_ref is None else start_ref[r : r + BLOCK, c : c + LANES]
            for t in range(half // LANES):
                got = jnp.where(tile == t, jnp.take_along_axis(table[t], at, axis=1), got)
            out_ref[r : r + BLOCK, c : c + LANES] = got


def far_kernel(where_ref, order_ref, data_ref, own_ref, idx_ref, out_ref,
               movie_ref, turned_ref, other_ref, final_ref):
    groups, pairs, rows, _ = data_ref.shape
    sources, side = own_ref.shape
    half = side // 2
    share = side // 8
    odd = where_ref[0]
    halo_cols = pl.ds(pl.multiple_of(odd * half, half), half)
    own_cols = pl.ds(pl.multiple_of(half - odd * half, half), half)
    tails = []
    for g in range(groups):
        for h in range(pairs):
            at = pl.ds((g * pairs + h) * rows, rows)
            movie_ref[at, halo_cols] = data_ref[g, h, :, :half].astype(F32)
            movie_ref[at, own_cols] = data_ref[g, h, :, half : 2 * half].astype(F32)
            tails.append(data_ref[g, h, :, 3 * half : 3 * half + LANES].astype(F32))
            frame = g + FAR * h
            for i in range(sources // rows):
                top, low = [
                    data_ref[g, h, :, pl.ds(3 * half + LANES + (n * (sources // rows) + i) * share, share)].astype(F32)
                    for n in range(2)
                ]
                other_ref[i * rows : (i + 1) * rows, frame * share : (frame + 1) * share] = top + low
    both_sweeps(order_ref, tails, movie_ref, turned_ref, own_ref, other_ref, final_ref)
    pick(final_ref, idx_ref, out_ref, odd * side, 0, None)


def near_side_kernel(where_ref, order_ref, data_ref, halo_ref, own_ref, idx_ref, start_ref, out_ref,
                     movie_ref, turned_ref, final_ref, other_ref):
    groups, pairs, rows, _ = data_ref.shape
    sources, side = own_ref.shape
    half = side // 2
    odd = where_ref[0]
    own_cols = pl.ds(pl.multiple_of(odd * half, half), half)
    halo_cols = pl.ds(pl.multiple_of(half - odd * half, half), half)
    lane = lax.broadcasted_iota(jnp.int32, (rows, LANES), 1)
    tails = []
    for g in range(groups):
        for h in range(pairs):
            at = pl.ds((g * pairs + h) * rows, rows)
            movie_ref[at, halo_cols] = halo_ref[g, h, :, :half]
            share = side // groups
            other_ref[h * rows : (h + 1) * rows, g * share : (g + 1) * share] = halo_ref[g, h, :, half + LANES :]
            movie_ref[at, own_cols] = data_ref[g, h, :, 2 * half : 3 * half].astype(F32)
            tails.append(
                jnp.where(
                    lane < sources,
                    halo_ref[g, h, :, half : half + LANES],
                    data_ref[g, h, :, 3 * half : 3 * half + LANES].astype(F32),
                )
            )
    both_sweeps(order_ref, tails, movie_ref, turned_ref, own_ref, other_ref, final_ref)
    pick(final_ref, idx_ref, out_ref, odd * side, side // LANES, start_ref)


def local(sizes, movie, traces, voxel_index, footprint, block_order):
    frames, slabs = sizes
    both = ("frames", "slabs")
    rows, voxels = movie.shape
    half = voxels // 2
    sources = traces.shape[1]
    side = voxels
    slab = lax.axis_index("slabs").astype(jnp.int32)
    odd = lax.rem(slab, 2)
    live = jnp.where((slab == 0) | (slab == slabs - 1), 0, 1).astype(jnp.int32)
    where = jnp.stack([odd, lax.axis_index("frames").astype(jnp.int32), live])
    wide = half + LANES + 4 * (side // 8)
    out, own_far, own_near = call(
        front_kernel,
        [jax.ShapeDtypeStruct((FAR, rows, wide), BF16)] + [jax.ShapeDtypeStruct((sources, side), F32)] * 2,
        [where], [voxel_index, footprint, movie, traces],
        [pltpu.VMEM((sources * 2 * side // LANES, LANES), F32)], limit=60,
    )
    got = lax.all_to_all(
        out, both, 0, 0,
        axis_index_groups=[
            [f * slabs + s % slabs for s in (a, a + 1) for f in (low, low + FAR)]
            for low in range(FAR) for a in range(1, slabs + 1, 2)
        ],
    )
    on_chip = [(f * slabs + s, f * slabs + (s ^ 1)) for f in range(frames) for s in range(slabs)]
    sent = call(middle_kernel, jax.ShapeDtypeStruct((FAR, 2, rows, wide + 2 * half), BF16), [where], [got])
    data = lax.all_to_all(
        sent, "frames", 0, 0,
        axis_index_groups=[list(range(a, a + FAR)) for a in range(0, frames, FAR)],
    )
    halo = lax.ppermute(
        call(
            near_kernel, jax.ShapeDtypeStruct((FAR, 2, rows, half + LANES + side // FAR), F32), [],
            [data, own_near],
        ),
        both, on_chip,
    )
    scratch = [pltpu.VMEM((frames * rows, side), F32), pltpu.VMEM((LANES, frames * rows), F32)]
    dense = pltpu.VMEM((sources, side), F32)
    result = jax.ShapeDtypeStruct(voxel_index.shape, F32)
    part = call(far_kernel, result, [where, block_order], [data, own_far, voxel_index], scratch + [dense, dense])
    return call(
        near_side_kernel, result, [where, block_order],
        [data, halo, own_near, voxel_index, part], scratch + [dense, dense],
    )


def solution(mesh):
    sizes = (mesh.shape["frames"], mesh.shape["slabs"])
    in_specs = (P("frames", "slabs"), P("frames", "slabs"), P("slabs", None), P("slabs", None), P())
    return jax.shard_map(
        functools.partial(local, sizes), mesh=mesh, in_specs=in_specs,
        out_specs=P("slabs", None), check_vma=False,
    )
```

```python
import functools

import jax
import jax.numpy as jnp
from jax import lax
from jax.experimental import pallas as pl
from jax.experimental.pallas import tpu as pltpu
from jax.sharding import PartitionSpec as P

F32 = jnp.float32
BF16 = jnp.bfloat16
BLOCK = 8
LANES = 128
FAR = 4


def call(body, out_shape, scalars, arrays, scratch=(), limit=16):
    vmem = pl.BlockSpec(memory_space=pltpu.VMEM)
    smem = pl.BlockSpec(memory_space=pltpu.SMEM)
    return pl.pallas_call(
        body,
        out_shape=out_shape,
        in_specs=[smem] * len(scalars) + [vmem] * len(arrays),
        out_specs=jax.tree.map(lambda _: vmem, out_shape),
        scratch_shapes=list(scratch),
        compiler_params=pltpu.CompilerParams(vmem_limit_bytes=limit << 20),
    )(*scalars, *arrays)


def place():
    slab = lax.axis_index("slabs")
    last = lax.axis_size("slabs") - 1
    live = jnp.where((slab == 0) | (slab == last), 0, 1)
    return lax.rem(slab, 2), lax.axis_index("frames"), live


def thirds(x):
    top = x.astype(BF16).astype(F32)
    rest = x - top
    mid = rest.astype(BF16).astype(F32)
    return top, mid, rest - mid


def front_kernel(idx_ref, val_ref, movie_ref, traces_ref, out_ref, far_ref, near_ref, rows_ref):
    sources, count = idx_ref.shape
    tiles = 2 * far_ref.shape[1] // LANES
    odd, frame, _ = place()
    tile_ids = lax.broadcasted_iota(jnp.int32, (tiles, count), 0).astype(F32).astype(BF16)
    lane_ids = lax.broadcasted_iota(jnp.int32, (LANES, count), 0).astype(F32).astype(BF16)
    one, none = jnp.ones((1, 1), BF16), jnp.zeros((1, 1), BF16)
    for k in range(sources):
        pos = idx_ref[k : k + 1, :]
        val = val_ref[k : k + 1, :]
        in_tile = tile_ids == (pos >> 7).astype(F32).astype(BF16)
        on_lane = jnp.where(lane_ids == (pos & (LANES - 1)).astype(F32).astype(BF16), one, none)
        left = jnp.concatenate(
            [jnp.where(in_tile, part.astype(BF16), none) for part in thirds(val) + (jnp.ones_like(val),)], axis=0
        )
        found = lax.dot_general(left, on_lane, (((1,), (1,)), ((), ())), preferred_element_type=F32)
        value = found[:tiles] + (found[tiles : 2 * tiles] + found[2 * tiles : 3 * tiles])
        rows_ref[k * tiles : (k + 1) * tiles, :] = jnp.where(found[3 * tiles :] > 0.5, value, -1.0)
    for t in range(tiles // 2):
        cols = slice(t * LANES, (t + 1) * LANES)
        left = rows_ref[pl.ds(t, sources, stride=tiles), :]
        right = rows_ref[pl.ds(t + tiles // 2, sources, stride=tiles), :]
        far_ref[:, cols] = jnp.where(odd == 1, right, left)
        near_ref[:, cols] = jnp.where(odd == 1, left, right)

    rows, voxels = movie_ref.shape
    half = voxels // 2
    share = far_ref.shape[1] // 8
    at = odd * half
    far_half = movie_ref[:, pl.ds(pl.multiple_of(at, half), half)]
    near_half = movie_ref[:, pl.ds(pl.multiple_of(half - at, half), half)]
    tail = jnp.concatenate(
        [traces_ref[...].astype(F32), jnp.zeros((rows, LANES - sources), F32)], axis=1
    ).astype(BF16)
    piece = far_ref[:, pl.ds(pl.multiple_of(frame * share, share), share)]
    parts = [p[r : r + rows].astype(BF16) for p in parts_of(piece) for r in range(0, sources, rows)]
    mine = 2 * (1 - odd)
    for h in range(2):
        for slot in (mine + h, 2 - mine + h):
            out_ref[slot, :, :half] = far_half
            out_ref[slot, :, half : half + LANES] = tail
        out_ref[mine + h, :, half + LANES : 2 * half + LANES] = near_half
        for i, part in enumerate(parts):
            out_ref[2 - mine + h, :, pl.ds(half + LANES + i * share, share)] = part


def middle_kernel(in_ref, out_ref):
    rows = in_ref.shape[1]
    half = (out_ref.shape[3] - in_ref.shape[2]) // 2
    odd, _, live = place()
    mine = 2 * (1 - odd)
    lane = lax.broadcasted_iota(jnp.int32, (rows, LANES), 1)
    for h in range(2):
        own, far = mine + h, 2 - mine + h
        far_half = in_ref[far, :, :half].astype(F32)
        far_half = jnp.where(live == 1, far_half, 0.0).astype(BF16)
        far_tail = jnp.where(live == 1, in_ref[far, :, half : half + LANES].astype(F32), 0.0)
        tail = (far_tail + pltpu.roll(in_ref[own, :, half : half + LANES].astype(F32), 16, 1)).astype(BF16)
        own_far = in_ref[own, :, :half]
        own_near = in_ref[own, :, half + LANES : 2 * half + LANES]
        dense = in_ref[far, :, half + LANES :]
        for g in range(FAR):
            out_ref[g, h, :, :half] = far_half
            out_ref[g, h, :, half : 2 * half] = own_far
            out_ref[g, h, :, 2 * half : 3 * half] = own_near
            out_ref[g, h, :, 3 * half : 3 * half + LANES] = tail
            out_ref[g, h, :, 3 * half + LANES :] = dense


def near_kernel(data_ref, dense_ref, out_ref):
    groups, pairs, rows, width = out_ref.shape
    sources, side = dense_ref.shape
    half = side // 2
    share = width - half - LANES
    for g in range(groups):
        for h in range(pairs):
            out_ref[g, h, :, :half] = data_ref[g, h, :, 2 * half : 3 * half].astype(F32)
            tail = data_ref[g, h, :, 3 * half : 3 * half + LANES].astype(F32)
            out_ref[g, h, :, half : half + LANES] = pltpu.roll(tail, LANES - 16, 1)
            out_ref[g, h, :, half + LANES :] = dense_ref[h * rows : (h + 1) * rows, g * share : (g + 1) * share]


def parts_of(x):
    top = x.astype(BF16).astype(F32)
    return top, x - top


def weights(g):
    top, low = parts_of(g)
    packed = top + pltpu.roll(low, 32, 1) + pltpu.roll(top, 64, 1) + pltpu.roll(low, 96, 1)
    return packed.astype(BF16)


def pull(packed, x):
    top, low = parts_of(x)
    top, low = top.astype(BF16), low.astype(BF16)
    stacked = jnp.concatenate([top, top, low, low], axis=0)
    return jnp.dot(packed, stacked, preferred_element_type=F32)


def both_sweeps(order_ref, tails, movie_ref, turned_ref, own_ref, other_ref, final_ref):
    sources = own_ref.shape[0]
    frames = movie_ref.shape[0]
    turned_ref[...] = jnp.transpose(jnp.concatenate(tails, axis=0))
    first = pl.multiple_of(order_ref[0] * BLOCK, BLOCK)
    second = pl.multiple_of(order_ref[1] * BLOCK, BLOCK)
    turned = jnp.concatenate(
        [turned_ref[pl.ds(base + at, BLOCK), :] for base in (0, sources) for at in (first, second)]
        + [jnp.zeros((LANES - 2 * sources, frames), F32)],
        axis=0,
    ).astype(BF16)
    gram = lax.dot_general(turned, turned, (((1,), (1,)), ((), ())), preferred_element_type=F32)[: 2 * sources]
    here = lax.broadcasted_iota(jnp.int32, gram.shape, 0)
    there = lax.broadcasted_iota(jnp.int32, gram.shape, 1)
    inverse = 1.0 / (jnp.sum(jnp.where(here == there, gram, 0.0), axis=1, keepdims=True) + 1.0)
    packed = weights(gram)
    inside = weights(jnp.where(here // sources == there // sources, gram, 0.0))
    stat = jnp.dot(turned[: 2 * sources], movie_ref[...].astype(BF16), preferred_element_type=F32)

    def cut(a):
        return [a[i * BLOCK : (i + 1) * BLOCK] for i in range(a.shape[0] // BLOCK)]

    raw = [ref[pl.ds(at, BLOCK), :] for ref in (other_ref, own_ref) for at in (first, second)]
    held = [r >= 0.0 for r in raw]
    x = [jnp.maximum(r, 0.0) for r in raw]
    s, v = cut(stat), cut(inverse)
    zero = jnp.zeros_like(x[0])

    def fresh(i, old, pulled):
        return jnp.where(held[i], jnp.maximum(old + (s[i] - pulled) * v[i], 0.0), 0.0)

    p = cut(pull(packed, jnp.concatenate(x, axis=0)))
    new = list(x)
    for i in (0, 2):
        new[i] = fresh(i, x[i], p[i])
    more = cut(pull(inside, jnp.concatenate([new[0] - x[0], zero, new[2] - x[2], zero], axis=0)))
    for i in (1, 3):
        new[i] = fresh(i, x[i], p[i] + more[i])
    p = cut(pull(packed[2 * BLOCK :], jnp.concatenate(new, axis=0)))
    last = fresh(2, new[2], p[0])
    more = pull(inside[3 * BLOCK :], jnp.concatenate([zero, zero, last - new[2], zero], axis=0))
    final = fresh(3, new[3], p[1] + more)
    final_ref[pl.ds(first, BLOCK), :] = last
    final_ref[pl.ds(second, BLOCK), :] = final


def pick(final_ref, idx_ref, out_ref, flip, base, start_ref):
    sources, half = final_ref.shape
    for r in range(0, sources, BLOCK):
        table = [final_ref[r : r + BLOCK, t * LANES : (t + 1) * LANES] for t in range(half // LANES)]
        for c in range(0, idx_ref.shape[1], LANES):
            pos = idx_ref[r : r + BLOCK, c : c + LANES] ^ flip
            tile = (pos >> 7) - base
            at = pos & (LANES - 1)
            got = jnp.zeros((BLOCK, LANES), F32) if start_ref is None else start_ref[r : r + BLOCK, c : c + LANES]
            for t in range(half // LANES):
                got = jnp.where(tile == t, jnp.take_along_axis(table[t], at, axis=1), got)
            out_ref[r : r + BLOCK, c : c + LANES] = got


def far_kernel(order_ref, data_ref, own_ref, idx_ref, out_ref,
               movie_ref, turned_ref, other_ref, final_ref):
    groups, pairs, rows, _ = data_ref.shape
    sources, side = own_ref.shape
    half = side // 2
    share = side // 8
    odd, _, _ = place()
    halo_cols = pl.ds(pl.multiple_of(odd * half, half), half)
    own_cols = pl.ds(pl.multiple_of(half - odd * half, half), half)
    tails = []
    for g in range(groups):
        for h in range(pairs):
            at = pl.ds((g * pairs + h) * rows, rows)
            movie_ref[at, halo_cols] = data_ref[g, h, :, :half].astype(F32)
            movie_ref[at, own_cols] = data_ref[g, h, :, half : 2 * half].astype(F32)
            tails.append(data_ref[g, h, :, 3 * half : 3 * half + LANES].astype(F32))
            frame = g + FAR * h
            for i in range(sources // rows):
                top, low = [
                    data_ref[g, h, :, pl.ds(3 * half + LANES + (n * (sources // rows) + i) * share, share)].astype(F32)
                    for n in range(2)
                ]
                other_ref[i * rows : (i + 1) * rows, frame * share : (frame + 1) * share] = top + low
    both_sweeps(order_ref, tails, movie_ref, turned_ref, own_ref, other_ref, final_ref)
    pick(final_ref, idx_ref, out_ref, odd * side, 0, None)


def near_side_kernel(order_ref, data_ref, halo_ref, own_ref, idx_ref, start_ref, out_ref,
                     movie_ref, turned_ref, final_ref, other_ref):
    groups, pairs, rows, _ = data_ref.shape
    sources, side = own_ref.shape
    half = side // 2
    odd, _, _ = place()
    own_cols = pl.ds(pl.multiple_of(odd * half, half), half)
    halo_cols = pl.ds(pl.multiple_of(half - odd * half, half), half)
    lane = lax.broadcasted_iota(jnp.int32, (rows, LANES), 1)
    tails = []
    for g in range(groups):
        for h in range(pairs):
            at = pl.ds((g * pairs + h) * rows, rows)
            movie_ref[at, halo_cols] = halo_ref[g, h, :, :half]
            share = side // groups
            other_ref[h * rows : (h + 1) * rows, g * share : (g + 1) * share] = halo_ref[g, h, :, half + LANES :]
            movie_ref[at, own_cols] = data_ref[g, h, :, 2 * half : 3 * half].astype(F32)
            tails.append(
                jnp.where(
                    lane < sources,
                    halo_ref[g, h, :, half : half + LANES],
                    data_ref[g, h, :, 3 * half : 3 * half + LANES].astype(F32),
                )
            )
    both_sweeps(order_ref, tails, movie_ref, turned_ref, own_ref, other_ref, final_ref)
    pick(final_ref, idx_ref, out_ref, odd * side, side // LANES, start_ref)


def local(sizes, movie, traces, voxel_index, footprint, block_order):
    frames, slabs = sizes
    both = ("frames", "slabs")
    rows, voxels = movie.shape
    half = voxels // 2
    sources = traces.shape[1]
    side = voxels
    wide = half + LANES + 4 * (side // 8)
    out, own_far, own_near = call(
        front_kernel,
        [jax.ShapeDtypeStruct((FAR, rows, wide), BF16)] + [jax.ShapeDtypeStruct((sources, side), F32)] * 2,
        [], [voxel_index, footprint, movie, traces],
        [pltpu.VMEM((sources * 2 * side // LANES, LANES), F32)], limit=60,
    )
    got = lax.all_to_all(
        out, both, 0, 0,
        axis_index_groups=[
            [f * slabs + s % slabs for s in (a, a + 1) for f in (low, low + FAR)]
            for low in range(FAR) for a in range(1, slabs + 1, 2)
        ],
    )
    on_chip = [(f * slabs + s, f * slabs + (s ^ 1)) for f in range(frames) for s in range(slabs)]
    sent = call(middle_kernel, jax.ShapeDtypeStruct((FAR, 2, rows, wide + 2 * half), BF16), [], [got])
    data = lax.all_to_all(
        sent, "frames", 0, 0,
        axis_index_groups=[list(range(a, a + FAR)) for a in range(0, frames, FAR)],
    )
    halo = lax.ppermute(
        call(
            near_kernel, jax.ShapeDtypeStruct((FAR, 2, rows, half + LANES + side // FAR), F32), [],
            [data, own_near],
        ),
        both, on_chip,
    )
    scratch = [pltpu.VMEM((frames * rows, side), F32), pltpu.VMEM((LANES, frames * rows), F32)]
    dense = pltpu.VMEM((sources, side), F32)
    result = jax.ShapeDtypeStruct(voxel_index.shape, F32)
    part = call(far_kernel, result, [block_order], [data, own_far, voxel_index], scratch + [dense, dense])
    return call(
        near_side_kernel, result, [block_order],
        [data, halo, own_near, voxel_index, part], scratch + [dense, dense],
    )


def solution(mesh):
    sizes = (mesh.shape["frames"], mesh.shape["slabs"])
    in_specs = (P("frames", "slabs"), P("frames", "slabs"), P("slabs", None), P("slabs", None), P())
    return jax.shard_map(
        functools.partial(local, sizes), mesh=mesh, in_specs=in_specs,
        out_specs=P("slabs", None), check_vma=False,
    )
```

```python
import functools

import jax
import jax.numpy as jnp
from jax import lax
from jax.experimental import pallas as pl
from jax.experimental.pallas import tpu as pltpu
from jax.sharding import PartitionSpec as P

F32 = jnp.float32
BF16 = jnp.bfloat16
BLOCK = 8
LANES = 128
FAR = 4
CROSS = 2


def call(body, out_shape, scalars, arrays, scratch=(), limit=16):
    vmem = pl.BlockSpec(memory_space=pltpu.VMEM)
    smem = pl.BlockSpec(memory_space=pltpu.SMEM)
    return pl.pallas_call(
        body,
        out_shape=out_shape,
        in_specs=[smem] * len(scalars) + [vmem] * len(arrays),
        out_specs=jax.tree.map(lambda _: vmem, out_shape),
        scratch_shapes=list(scratch),
        compiler_params=pltpu.CompilerParams(vmem_limit_bytes=limit << 20),
    )(*scalars, *arrays)


def place():
    slab = lax.axis_index("slabs")
    last = lax.axis_size("slabs") - 1
    live = jnp.where((slab == 0) | (slab == last), 0, 1)
    return lax.rem(slab, 2), lax.axis_index("frames"), live


def thirds(x):
    top = x.astype(BF16).astype(F32)
    rest = x - top
    mid = rest.astype(BF16).astype(F32)
    return top, mid, rest - mid


def front_kernel(idx_ref, val_ref, movie_ref, traces_ref, out_ref, far_ref, near_ref, rows_ref):
    sources, count = idx_ref.shape
    tiles = 2 * far_ref.shape[1] // LANES
    odd, frame, _ = place()
    tile_ids = lax.broadcasted_iota(jnp.int32, (tiles, count), 0).astype(F32).astype(BF16)
    lane_ids = lax.broadcasted_iota(jnp.int32, (LANES, count), 0).astype(F32).astype(BF16)
    one, none = jnp.ones((1, 1), BF16), jnp.zeros((1, 1), BF16)
    for k in range(sources):
        pos = idx_ref[k : k + 1, :]
        val = val_ref[k : k + 1, :]
        in_tile = tile_ids == (pos >> 7).astype(F32).astype(BF16)
        on_lane = jnp.where(lane_ids == (pos & (LANES - 1)).astype(F32).astype(BF16), one, none)
        left = jnp.concatenate(
            [jnp.where(in_tile, part.astype(BF16), none) for part in thirds(val) + (jnp.ones_like(val),)], axis=0
        )
        found = lax.dot_general(left, on_lane, (((1,), (1,)), ((), ())), preferred_element_type=F32)
        value = found[:tiles] + (found[tiles : 2 * tiles] + found[2 * tiles : 3 * tiles])
        rows_ref[k * tiles : (k + 1) * tiles, :] = jnp.where(found[3 * tiles :] > 0.5, value, -1.0)
    for t in range(tiles // 2):
        cols = slice(t * LANES, (t + 1) * LANES)
        left = rows_ref[pl.ds(t, sources, stride=tiles), :]
        right = rows_ref[pl.ds(t + tiles // 2, sources, stride=tiles), :]
        far_ref[:, cols] = jnp.where(odd == 1, right, left)
        near_ref[:, cols] = jnp.where(odd == 1, left, right)

    rows, voxels = movie_ref.shape
    half = voxels // 2
    share = far_ref.shape[1] // 8
    at = odd * half
    far_half = movie_ref[:, pl.ds(pl.multiple_of(at, half), half)]
    near_half = movie_ref[:, pl.ds(pl.multiple_of(half - at, half), half)]
    tail = jnp.concatenate(
        [traces_ref[...].astype(F32), jnp.zeros((rows, LANES - sources), F32)], axis=1
    ).astype(BF16)
    piece = far_ref[:, pl.ds(pl.multiple_of(frame * share, share), share)]
    parts = [p[r : r + rows].astype(BF16) for p in parts_of(piece) for r in range(0, sources, rows)]
    mine = 2 * (1 - odd)
    for h in range(2):
        for slot in (mine + h, 2 - mine + h):
            out_ref[slot, :, :half] = far_half
            out_ref[slot, :, half : half + LANES] = tail
        out_ref[mine + h, :, half + LANES : 2 * half + LANES] = near_half
        for i, part in enumerate(parts):
            out_ref[2 - mine + h, :, pl.ds(half + LANES + i * share, share)] = part


def middle_kernel(in_ref, out_ref):
    rows = in_ref.shape[1]
    half = (out_ref.shape[3] - in_ref.shape[2]) // 2
    odd, _, live = place()
    mine = 2 * (1 - odd)
    lane = lax.broadcasted_iota(jnp.int32, (rows, LANES), 1)
    for h in range(2):
        own, far = mine + h, 2 - mine + h
        far_half = in_ref[far, :, :half].astype(F32)
        far_half = jnp.where(live == 1, far_half, 0.0).astype(BF16)
        far_tail = jnp.where(live == 1, in_ref[far, :, half : half + LANES].astype(F32), 0.0)
        tail = (far_tail + pltpu.roll(in_ref[own, :, half : half + LANES].astype(F32), 16, 1)).astype(BF16)
        own_far = in_ref[own, :, :half]
        own_near = in_ref[own, :, half + LANES : 2 * half + LANES]
        dense = in_ref[far, :, half + LANES :]
        for g in range(FAR):
            out_ref[g, h, :, :half] = far_half
            out_ref[g, h, :, half : 2 * half] = own_far
            out_ref[g, h, :, 2 * half : 3 * half] = own_near
            out_ref[g, h, :, 3 * half : 3 * half + LANES] = tail
            out_ref[g, h, :, 3 * half + LANES :] = dense


def near_kernel(data_ref, dense_ref, out_ref):
    groups, pairs, rows, width = out_ref.shape
    sources, side = dense_ref.shape
    half = side // 2
    share = width - half - LANES
    for g in range(groups):
        for h in range(pairs):
            out_ref[g, h, :, :half] = data_ref[g, h, :, 2 * half : 3 * half].astype(F32)
            tail = data_ref[g, h, :, 3 * half : 3 * half + LANES].astype(F32)
            out_ref[g, h, :, half : half + LANES] = pltpu.roll(tail, LANES - 16, 1)
            out_ref[g, h, :, half + LANES :] = dense_ref[h * rows : (h + 1) * rows, g * share : (g + 1) * share]


def parts_of(x):
    top = x.astype(BF16).astype(F32)
    return top, x - top


def weights(g):
    top, low = parts_of(g)
    packed = top + pltpu.roll(low, 32, 1) + pltpu.roll(top, 64, 1) + pltpu.roll(low, 96, 1)
    return packed.astype(BF16)


def pull(packed, x):
    top, low = parts_of(x)
    top, low = top.astype(BF16), low.astype(BF16)
    stacked = jnp.concatenate([top, top, low, low], axis=0)
    return jnp.dot(packed, stacked, preferred_element_type=F32)


def both_sweeps(order_ref, tails, movie_ref, turned_ref, own_ref, other_ref, final_ref):
    sources = own_ref.shape[0]
    frames = movie_ref.shape[0]
    turned_ref[...] = jnp.transpose(jnp.concatenate(tails, axis=0))
    first = pl.multiple_of(order_ref[0] * BLOCK, BLOCK)
    second = pl.multiple_of(order_ref[1] * BLOCK, BLOCK)
    turned = jnp.concatenate(
        [turned_ref[pl.ds(base + at, BLOCK), :] for base in (0, sources) for at in (first, second)]
        + [jnp.zeros((LANES - 2 * sources, frames), F32)],
        axis=0,
    ).astype(BF16)
    gram = lax.dot_general(turned, turned, (((1,), (1,)), ((), ())), preferred_element_type=F32)[: 2 * sources]
    here = lax.broadcasted_iota(jnp.int32, gram.shape, 0)
    there = lax.broadcasted_iota(jnp.int32, gram.shape, 1)
    inverse = 1.0 / (jnp.sum(jnp.where(here == there, gram, 0.0), axis=1, keepdims=True) + 1.0)
    packed = weights(gram)
    inside = weights(jnp.where(here // sources == there // sources, gram, 0.0))
    stat = jnp.dot(turned[: 2 * sources], movie_ref[...].astype(BF16), preferred_element_type=F32)

    def cut(a):
        return [a[i * BLOCK : (i + 1) * BLOCK] for i in range(a.shape[0] // BLOCK)]

    raw = [ref[pl.ds(at, BLOCK), :] for ref in (other_ref, own_ref) for at in (first, second)]
    held = [r >= 0.0 for r in raw]
    x = [jnp.maximum(r, 0.0) for r in raw]
    s, v = cut(stat), cut(inverse)
    zero = jnp.zeros_like(x[0])

    def fresh(i, old, pulled):
        return jnp.where(held[i], jnp.maximum(old + (s[i] - pulled) * v[i], 0.0), 0.0)

    p = cut(pull(packed, jnp.concatenate(x, axis=0)))
    new = list(x)
    for i in (0, 2):
        new[i] = fresh(i, x[i], p[i])
    more = cut(pull(inside, jnp.concatenate([new[0] - x[0], zero, new[2] - x[2], zero], axis=0)))
    for i in (1, 3):
        new[i] = fresh(i, x[i], p[i] + more[i])
    p = cut(pull(packed[2 * BLOCK :], jnp.concatenate(new, axis=0)))
    last = fresh(2, new[2], p[0])
    more = pull(inside[3 * BLOCK :], jnp.concatenate([zero, zero, last - new[2], zero], axis=0))
    final = fresh(3, new[3], p[1] + more)
    final_ref[pl.ds(first, BLOCK), :] = last
    final_ref[pl.ds(second, BLOCK), :] = final


def pick(final_ref, idx_ref, out_ref, flip, base, start_ref):
    sources, half = final_ref.shape
    for r in range(0, sources, BLOCK):
        table = [final_ref[r : r + BLOCK, t * LANES : (t + 1) * LANES] for t in range(half // LANES)]
        for c in range(0, idx_ref.shape[1], LANES):
            pos = idx_ref[r : r + BLOCK, c : c + LANES] ^ flip
            tile = (pos >> 7) - base
            at = pos & (LANES - 1)
            got = jnp.zeros((BLOCK, LANES), F32) if start_ref is None else start_ref[r : r + BLOCK, c : c + LANES]
            for t in range(half // LANES):
                got = jnp.where(tile == t, jnp.take_along_axis(table[t], at, axis=1), got)
            out_ref[r : r + BLOCK, c : c + LANES] = got


def far_kernel(order_ref, data_ref, own_ref, idx_ref, out_ref,
               movie_ref, turned_ref, other_ref, final_ref):
    groups, pairs, rows, _ = data_ref.shape
    sources, side = own_ref.shape
    half = side // 2
    share = side // 8
    odd, _, _ = place()
    halo_cols = pl.ds(pl.multiple_of(odd * half, half), half)
    own_cols = pl.ds(pl.multiple_of(half - odd * half, half), half)
    lane = lax.broadcasted_iota(jnp.int32, (rows, LANES), 1)
    tails = []
    for g in range(groups):
        for h in range(pairs):
            at = pl.ds((g * pairs + h) * rows, rows)
            far = g ^ CROSS
            movie_ref[at, halo_cols] = data_ref[far, h, :, :half].astype(F32)
            movie_ref[at, own_cols] = data_ref[g, h, :, half : 2 * half].astype(F32)
            tail = pl.ds(3 * half, LANES)
            tails.append(
                jnp.where(
                    lane < sources, data_ref[far, h, :, tail].astype(F32), data_ref[g, h, :, tail].astype(F32)
                )
            )
            frame = far + FAR * h
            for i in range(sources // rows):
                top, low = [
                    data_ref[g, h, :, pl.ds(3 * half + LANES + (n * (sources // rows) + i) * share, share)].astype(F32)
                    for n in range(2)
                ]
                other_ref[i * rows : (i + 1) * rows, frame * share : (frame + 1) * share] = top + low
    both_sweeps(order_ref, tails, movie_ref, turned_ref, own_ref, other_ref, final_ref)
    pick(final_ref, idx_ref, out_ref, odd * side, 0, None)


def near_side_kernel(order_ref, data_ref, halo_ref, own_ref, idx_ref, start_ref, out_ref,
                     movie_ref, turned_ref, final_ref, other_ref):
    groups, pairs, rows, _ = data_ref.shape
    sources, side = own_ref.shape
    half = side // 2
    odd, _, _ = place()
    own_cols = pl.ds(pl.multiple_of(odd * half, half), half)
    halo_cols = pl.ds(pl.multiple_of(half - odd * half, half), half)
    lane = lax.broadcasted_iota(jnp.int32, (rows, LANES), 1)
    tails = []
    for g in range(groups):
        for h in range(pairs):
            at = pl.ds((g * pairs + h) * rows, rows)
            movie_ref[at, halo_cols] = halo_ref[g, h, :, :half]
            share = side // groups
            other_ref[h * rows : (h + 1) * rows, g * share : (g + 1) * share] = halo_ref[g, h, :, half + LANES :]
            movie_ref[at, own_cols] = data_ref[g, h, :, 2 * half : 3 * half].astype(F32)
            tails.append(
                jnp.where(
                    lane < sources,
                    halo_ref[g, h, :, half : half + LANES],
                    data_ref[g, h, :, 3 * half : 3 * half + LANES].astype(F32),
                )
            )
    both_sweeps(order_ref, tails, movie_ref, turned_ref, own_ref, other_ref, final_ref)
    pick(final_ref, idx_ref, out_ref, odd * side, side // LANES, start_ref)


def local(sizes, movie, traces, voxel_index, footprint, block_order):
    frames, slabs = sizes
    both = ("frames", "slabs")
    rows, voxels = movie.shape
    half = voxels // 2
    sources = traces.shape[1]
    side = voxels
    wide = half + LANES + 4 * (side // 8)
    out, own_far, own_near = call(
        front_kernel,
        [jax.ShapeDtypeStruct((FAR, rows, wide), BF16)] + [jax.ShapeDtypeStruct((sources, side), F32)] * 2,
        [], [voxel_index, footprint, movie, traces],
        [pltpu.VMEM((sources * 2 * side // LANES, LANES), F32)], limit=60,
    )
    got = lax.all_to_all(
        out, both, 0, 0,
        axis_index_groups=[
            [f * slabs + s % slabs for s, at in ((a, low), (a + 1, low ^ CROSS)) for f in (at, at + FAR)]
            for low in range(FAR) for a in range(1, slabs + 1, 2)
        ],
    )
    on_chip = [(f * slabs + s, f * slabs + (s ^ 1)) for f in range(frames) for s in range(slabs)]
    sent = call(middle_kernel, jax.ShapeDtypeStruct((FAR, 2, rows, wide + 2 * half), BF16), [], [got])
    data = lax.all_to_all(
        sent, "frames", 0, 0,
        axis_index_groups=[list(range(a, a + FAR)) for a in range(0, frames, FAR)],
    )
    halo = lax.ppermute(
        call(
            near_kernel, jax.ShapeDtypeStruct((FAR, 2, rows, half + LANES + side // FAR), F32), [],
            [data, own_near],
        ),
        both, on_chip,
    )
    scratch = [pltpu.VMEM((frames * rows, side), F32), pltpu.VMEM((LANES, frames * rows), F32)]
    dense = pltpu.VMEM((sources, side), F32)
    result = jax.ShapeDtypeStruct(voxel_index.shape, F32)
    part = call(far_kernel, result, [block_order], [data, own_far, voxel_index], scratch + [dense, dense])
    return call(
        near_side_kernel, result, [block_order],
        [data, halo, own_near, voxel_index, part], scratch + [dense, dense],
    )


def solution(mesh):
    sizes = (mesh.shape["frames"], mesh.shape["slabs"])
    in_specs = (P("frames", "slabs"), P("frames", "slabs"), P("slabs", None), P("slabs", None), P())
    return jax.shard_map(
        functools.partial(local, sizes), mesh=mesh, in_specs=in_specs,
        out_specs=P("slabs", None), check_vma=False,
    )
```
